32 devices in a mesh: tm: 4 (over y, core), space: 8 (over z, x).
Axes of the slice: x: 2, y: 2, z: 4, core: 2. Of those that a mesh axis runs over, the one named last changes fastest.
Arguments:
- first_state: float32 [16, 64, 256], P(None, 'space'), may hold values from -6 to 6
- time_embed: float32 [4, 320], P('tm'), may hold values from -6 to 6
- drift_scale: float32 [4], P('tm'), may hold values from 0.05 to 0.25
- state_decay: float32 [4], P('tm'), may hold values from 0.01 to 0.1
- lift_weight: bfloat16 [320, 16], replicated, may hold values from -1.5 to 1.5
- conv_one: bfloat16 [3, 3, 320, 320], replicated, may hold values from -0.109375 to 0.109375
- conv_two: bfloat16 [3, 3, 320, 320], replicated, may hold values from -0.109375 to 0.109375
- project_weight: bfloat16 [16, 320], replicated, may hold values from -0.3125 to 0.3125
Outputs:
- trajectory: float32 [4, 16, 64, 256], P('tm', None, 'space')
The draws below stay inside these ranges and needn't reach their ends.
All inputs are finite; a program needn't handle non-finite values.
Results may differ from the reference program's by a relative error of at most 0.0019.
Values may be sent and summed in bfloat16 or wider, within the bound.
A program may use at most 128 MiB of HBM per device.

```python
import math
import jax
import jax.numpy as jnp
from jax import lax

C = 16
F = 320
W = 256
ITERS = 2
H = 64
STEPS = 4


def shard_levels(own_key, dims, shards, least, high):
    gain = 1.0
    for position, parts in shards:
        heights = jax.random.uniform(jax.random.fold_in(jax.random.fold_in(own_key, 6), position), (parts,), jnp.float32, least / len(shards), high / len(shards))
        gain = gain * jnp.repeat(jnp.exp(heights), dims[position] // parts).reshape((-1,) + (1,) * (len(dims) - 1 - position))
    return gain


def scatter_about(own_key, extent, scale, most, pieces=(), kind=jnp.bfloat16):
    array = jax.random.normal(own_key, extent, jnp.float32) * scale
    if len(pieces) > 0:
        array = shard_levels(own_key, extent, pieces, -0.22, 0.18) * array
    return jnp.clip(array, min=-most, max=most).astype(kind)


def setup_inputs(seed: int = 0) -> dict:
    key_of = jax.random.split(jax.random.key(seed), 9)
    return {
        "first_state": scatter_about(key_of[0], (C, H, W), 1.0, 6.0, ((1, 8),), jnp.float32),
        "time_embed": scatter_about(key_of[1], (STEPS, F), 1.0, 6.0, ((0, 4),), jnp.float32),
        "drift_scale": jnp.clip(jnp.exp(math.log(0.25) - 1.609438 * jax.random.uniform(key_of[2], (STEPS,), jnp.float32) ** shard_levels(key_of[2], (STEPS,), ((0, 4),), -0.2, 0.2)), 0.05, 0.25),
        "state_decay": jnp.clip(jnp.exp(math.log(0.1) - 2.3025851 * jax.random.uniform(key_of[3], (STEPS,), jnp.float32) ** shard_levels(key_of[3], (STEPS,), ((0, 4),), -0.2, 0.2)), 0.01, 0.1),
        "lift_weight": scatter_about(key_of[4], (F, C), C ** -0.5, 1.5),
        "conv_one": scatter_about(key_of[5], (3, 3, F, F), (9 * F) ** -0.5, 0.109375),
        "conv_two": scatter_about(key_of[6], (3, 3, F, F), (9 * F) ** -0.5, 0.109375),
        "project_weight": scatter_about(key_of[7], (C, F), F ** -0.5, 0.3125),
    }


def shift_columns(field, col_tap):
    spread = [(0, 0)] * (field.ndim - 1)
    if col_tap == 0:
        return jnp.pad(field[..., :-1], spread + [(1, 0)])
    if col_tap == 2:
        return jnp.pad(field[..., 1:], spread + [(0, 1)])
    return field


def convolve(active, weight):
    chans, height, width = active.shape
    padded = jnp.pad(active, ((0, 0), (1, 1), (0, 0)))
    total = jnp.zeros((weight.shape[2], height * width), jnp.float32)
    for row_tap in range(3):
        rows_view = padded[:, row_tap:row_tap + height]
        for col_tap in range(3):
            tile = shift_columns(rows_view, col_tap).reshape(chans, -1)
            total = total + jnp.dot(weight[row_tap, col_tap], tile, preferred_element_type=jnp.float32)
    return total.reshape(-1, height, width)


def denoise_one(state, embed, lift_weight, conv_one, conv_two, project_weight):
    chans, height, width = state.shape
    flat = state.astype(jnp.bfloat16).reshape(chans, -1)
    lifted = jnp.dot(lift_weight, flat, preferred_element_type=jnp.float32).reshape(-1, height, width)
    lifted = lifted + embed[:, None, None]
    first = lifted + convolve(jax.nn.silu(lifted).astype(jnp.bfloat16), conv_one)
    second = first + convolve(jax.nn.silu(first).astype(jnp.bfloat16), conv_two)
    active = jax.nn.silu(second).astype(jnp.bfloat16).reshape(second.shape[0], -1)
    return jnp.dot(project_weight, active, preferred_element_type=jnp.float32).reshape(chans, height, width)


def reference(first_state, time_embed, drift_scale, state_decay, lift_weight, conv_one, conv_two, project_weight):
    states = jnp.broadcast_to(first_state[None], (STEPS,) + first_state.shape)
    running = jnp.zeros_like(states)
    for sweep in range(ITERS):
        def single(pair):
            return denoise_one(pair[0], pair[1], lift_weight, conv_one, conv_two, project_weight)

        outputs = lax.map(single, (states, time_embed))
        drifts = drift_scale[:, None, None, None] * outputs - state_decay[:, None, None, None] * states
        running = jnp.cumsum(drifts, axis=0)
        if sweep + 1 < ITERS:
            shifted = jnp.concatenate([jnp.zeros_like(running[:1]), running[:-1]], axis=0)
            states = first_state[None] + shifted
    return first_state[None] + running
```

```python
import functools

import jax
import jax.numpy as jnp
from jax import lax
from jax.experimental import pallas as pl
from jax.experimental.pallas import tpu as pltpu
from jax.sharding import PartitionSpec as P

ITERS = 2
MESH = pl.DeviceIdType.MESH


def silu(v):
    half = 0.5 * v
    return half + half * jnp.tanh(half)


def kernel(
    steps,
    tiles,
    x_ref,
    embed_ref,
    scale_ref,
    decay_ref,
    lift_ref,
    project_ref,
    conv_one_ref,
    conv_two_ref,
    out_ref,
    raw_one,
    raw_two,
    w_one,
    w_two,
    embed_bc,
    cols_one,
    cols_two,
    first,
    rows_f32,
    state_rows,
    xb_rows,
    halo_out,
    halo_in,
    drift_out,
    drift_in,
    w_sem,
    halo_send,
    halo_recv,
    drift_send,
    drift_recv,
):
    chans, height, width = x_ref.shape
    feats = lift_ref.shape[0]
    block = 3 * feats
    depth = 3 * block
    tm = lax.axis_index("tm")
    space = lax.axis_index("space")
    has_up = space > 0
    has_down = space < tiles - 1

    load_one = pltpu.make_async_copy(conv_one_ref, raw_one, w_sem.at[0])
    load_two = pltpu.make_async_copy(conv_two_ref, raw_two, w_sem.at[1])
    load_one.start()
    load_two.start()

    barrier = pltpu.get_barrier_semaphore()
    for shift in range(1, steps):
        other = lax.rem(tm + shift, steps)
        pl.semaphore_signal(barrier, inc=1, device_id=(other, space), device_id_type=MESH)

    @pl.when(has_up)
    def _():
        pl.semaphore_signal(barrier, inc=1, device_id=(tm, space - 1), device_id_type=MESH)

    @pl.when(has_down)
    def _():
        pl.semaphore_signal(barrier, inc=1, device_id=(tm, space + 1), device_id_type=MESH)

    def halo_copies(sweep):
        up = pltpu.make_async_remote_copy(
            src_ref=halo_out.at[sweep, 0],
            dst_ref=halo_in.at[sweep, 1],
            send_sem=halo_send.at[sweep, 0],
            recv_sem=halo_recv.at[sweep, 1],
            device_id=(tm, space - 1),
            device_id_type=MESH,
        )
        down = pltpu.make_async_remote_copy(
            src_ref=halo_out.at[sweep, 1],
            dst_ref=halo_in.at[sweep, 0],
            send_sem=halo_send.at[sweep, 1],
            recv_sem=halo_recv.at[sweep, 0],
            device_id=(tm, space + 1),
            device_id_type=MESH,
        )
        return up, down

    def send_halo(sweep):
        up, down = halo_copies(sweep)

        @pl.when(has_up)
        def _():
            up.start()

        @pl.when(has_down)
        def _():
            down.start()

    def wait_halo(sweep):
        up, down = halo_copies(sweep)

        @pl.when(has_up)
        def _():
            down.wait_recv()

        @pl.when(has_down)
        def _():
            up.wait_recv()

    def drift_copy(sweep, shift, row):
        return pltpu.make_async_remote_copy(
            src_ref=drift_out.at[sweep, row],
            dst_ref=drift_in.at[sweep, shift - 1, row],
            send_sem=drift_send.at[sweep, shift - 1, row],
            recv_sem=drift_recv.at[sweep, shift - 1, row],
            device_id=(tm + shift, space),
            device_id_type=MESH,
        )

    def send_drift(sweep, row):
        for shift in range(1, steps):

            @pl.when(tm + shift < steps)
            def _():
                drift_copy(sweep, shift, row).start()

    def earlier(sweep, row):
        total = jnp.zeros((chans, width), jnp.float32)
        for shift in range(1, steps):

            @pl.when(tm >= shift)
            def _():
                drift_copy(sweep, shift, row).wait_recv()

            total = total + jnp.where(tm >= shift, drift_in[sweep, shift - 1, row], 0.0)
        return total

    lane = lax.broadcasted_iota(jnp.int32, (feats, width), 1)

    def store_columns(cols, index, act):
        base = pl.multiple_of(index * block, 64)
        left = jnp.where(lane == 0, 0.0, pltpu.roll(act, 1, 1))
        right = jnp.where(lane == width - 1, 0.0, pltpu.roll(act, width - 1, 1))
        cols[pl.ds(base, feats), :] = left.astype(jnp.bfloat16)
        cols[pl.ds(base + feats, feats), :] = act.astype(jnp.bfloat16)
        cols[pl.ds(base + 2 * feats, feats), :] = right.astype(jnp.bfloat16)

    def lift(xb):
        value = jnp.dot(lift_ref[...], xb, preferred_element_type=jnp.float32)
        return value + jnp.concatenate([embed_bc[...]] * (width // 128), axis=1)

    def conv(weight, cols, index):
        base = pl.multiple_of(index * block, 64)
        return jnp.dot(
            weight[...], cols[pl.ds(base, depth), :], preferred_element_type=jnp.float32
        )

    def own_row(row):
        lifted = lift(xb_rows[row])
        first[row + 1] = lifted
        store_columns(cols_one, row + 2, silu(lifted))

    def halo_row(sweep, side, step):
        inside = has_up if side == 0 else has_down
        lifted = lift(jnp.where(inside, halo_in[sweep, side, step], 0))
        if side == 0 and step == 1:
            first[0] = lifted
        if side == 1 and step == 0:
            first[height + 1] = lifted
        index = step if side == 0 else height + 2 + step
        store_columns(cols_one, index, jnp.where(inside, silu(lifted), 0.0))

    def conv_one_row(index, inside=None):
        value = first[index] + conv(w_one, cols_one, index)
        first[index] = value
        act = silu(value)
        if inside is not None:
            act = jnp.where(inside, act, 0.0)
        store_columns(cols_two, index, act)

    def conv_two_row(sweep, row):
        value = first[row + 1] + conv(w_two, cols_two, row)
        act = silu(value).astype(jnp.bfloat16)
        out = jnp.dot(project_ref[...], act, preferred_element_type=jnp.float32)
        drift_out[sweep, row] = scale_ref[0] * out - decay_ref[0] * state_rows[row]
        send_drift(sweep, row)

    def build_weight(raw, weight):
        for tap in range(9):
            weight[:, tap * feats : (tap + 1) * feats] = raw[tap // 3, tap % 3]

    for row in range(height):
        value = x_ref[:, row, :]
        rows_f32[row] = value
        state_rows[row] = value
        rounded = value.astype(jnp.bfloat16)
        xb_rows[row] = rounded
        if row < 2:
            halo_out[0, 0, row] = rounded
        if row >= height - 2:
            halo_out[0, 1, row - (height - 2)] = rounded
    embed_bc[...] = jnp.transpose(
        jnp.pad(jnp.broadcast_to(embed_ref[...], (128, feats)), ((0, 0), (0, (-feats) % 128)))
    )[:feats]

    greeted = (steps - 1) + jnp.where(has_up, 1, 0) + jnp.where(has_down, 1, 0)
    pl.semaphore_wait(barrier, greeted)
    send_halo(0)

    for sweep in range(ITERS):
        if sweep > 0:
            for row in (0, 1, height - 1, height - 2):
                state = rows_f32[row] + earlier(sweep - 1, row)
                state_rows[row] = state
                rounded = state.astype(jnp.bfloat16)
                xb_rows[row] = rounded
                if row < 2:
                    halo_out[sweep, 0, row] = rounded
                else:
                    halo_out[sweep, 1, row - (height - 2)] = rounded
            send_halo(sweep)

            @pl.loop(2, height - 2)
            def _(row):
                state = rows_f32[row] + earlier(sweep - 1, row)
                state_rows[row] = state
                xb_rows[row] = state.astype(jnp.bfloat16)

        @pl.loop(0, height)
        def _(row):
            own_row(row)

        if sweep == 0:
            load_one.wait()
            build_weight(raw_one, w_one)

        @pl.loop(2, height)
        def _(index):
            conv_one_row(index)

        wait_halo(sweep)
        for side in range(2):
            for step in range(2):
                halo_row(sweep, side, step)
        conv_one_row(1)
        conv_one_row(height)
        conv_one_row(0, has_up)
        conv_one_row(height + 1, has_down)

        if sweep == 0:
            load_two.wait()
            build_weight(raw_two, w_two)

        @pl.loop(0, height)
        def _(turn):
            row = jnp.where(turn < 2, turn, jnp.where(turn < 4, height + 1 - turn, turn - 2))
            conv_two_row(sweep, row)

    for row in range(height):
        total = drift_out[ITERS - 1, row] + earlier(ITERS - 1, row)
        out_ref[0, :, row, :] = rows_f32[row] + total

    for sweep in range(ITERS):
        up, down = halo_copies(sweep)

        @pl.when(has_up)
        def _():
            up.wait_send()

        @pl.when(has_down)
        def _():
            down.wait_send()

        for shift in range(1, steps):
            for row in range(height):

                @pl.when(tm + shift < steps)
                def _():
                    drift_copy(sweep, shift, row).wait_send()


def solution(mesh):
    steps, tiles = mesh.shape["tm"], mesh.shape["space"]

    def per_device(
        first_state,
        time_embed,
        drift_scale,
        state_decay,
        lift_weight,
        conv_one,
        conv_two,
        project_weight,
    ):
        chans, height, width = first_state.shape
        feats = lift_weight.shape[0]
        block, depth = 3 * feats, 9 * feats
        peers = max(steps - 1, 1)
        vmem = pl.BlockSpec(memory_space=pltpu.VMEM)
        smem = pl.BlockSpec(memory_space=pltpu.SMEM)
        hbm = pl.BlockSpec(memory_space=pl.ANY)
        return pl.pallas_call(
            functools.partial(kernel, steps, tiles),
            out_shape=jax.ShapeDtypeStruct((1, chans, height, width), jnp.float32),
            in_specs=[vmem, vmem, smem, smem, vmem, vmem, hbm, hbm],
            out_specs=vmem,
            scratch_shapes=[
                pltpu.VMEM((3, 3, feats, feats), jnp.bfloat16),
                pltpu.VMEM((3, 3, feats, feats), jnp.bfloat16),
                pltpu.VMEM((feats, depth), jnp.bfloat16),
                pltpu.VMEM((feats, depth), jnp.bfloat16),
                pltpu.VMEM((feats, 128), jnp.float32),
                pltpu.VMEM(((height + 4) * block, width), jnp.bfloat16),
                pltpu.VMEM(((height + 2) * block, width), jnp.bfloat16),
                pltpu.VMEM((height + 2, feats, width), jnp.float32),
                pltpu.VMEM((height, chans, width), jnp.float32),
                pltpu.VMEM((height, chans, width), jnp.float32),
                pltpu.VMEM((height, chans, width), jnp.bfloat16),
                pltpu.VMEM((ITERS, 2, 2, chans, width), jnp.bfloat16),
                pltpu.VMEM((ITERS, 2, 2, chans, width), jnp.bfloat16),
                pltpu.VMEM((ITERS, height, chans, width), jnp.float32),
                pltpu.VMEM((ITERS, peers, height, chans, width), jnp.float32),
                pltpu.SemaphoreType.DMA((2,)),
                pltpu.SemaphoreType.DMA((ITERS, 2)),
                pltpu.SemaphoreType.DMA((ITERS, 2)),
                pltpu.SemaphoreType.DMA((ITERS, peers, height)),
                pltpu.SemaphoreType.DMA((ITERS, peers, height)),
            ],
            compiler_params=pltpu.CompilerParams(
                collective_id=0, has_side_effects=True, vmem_limit_bytes=48 * 1024 * 1024
            ),
        )(
            first_state,
            time_embed,
            drift_scale,
            state_decay,
            lift_weight,
            project_weight,
            conv_one,
            conv_two,
        )

    in_specs = (P(None, "space", None), P("tm", None), P("tm"), P("tm"), P(), P(), P(), P())
    return jax.shard_map(
        per_device,
        mesh=mesh,
        in_specs=in_specs,
        out_specs=P("tm", None, "space", None),
        check_vma=False,
    )
```

```python
import functools

import jax
import jax.numpy as jnp
from jax import lax
from jax.experimental import pallas as pl
from jax.experimental.pallas import tpu as pltpu
from jax.sharding import PartitionSpec as P

ITERS = 2
MESH = pl.DeviceIdType.MESH


def silu(v):
    half = 0.5 * v
    return half + half * jnp.tanh(half)


def kernel(
    steps,
    tiles,
    x_hbm,
    embed_hbm,
    scale_ref,
    decay_ref,
    lift_hbm,
    project_hbm,
    conv_one_hbm,
    conv_two_hbm,
    out_ref,
    x_ref,
    embed_ref,
    lift_ref,
    project_ref,
    raw_one,
    raw_two,
    w_one,
    w_two,
    embed_bc,
    lift_rows,
    cols_one,
    cols_two,
    first,
    sums_one,
    sums_two,
    act_three,
    rows_f32,
    state_rows,
    xb_rows,
    drift_out,
    drift_in,
    load_sem,
    halo_send,
    halo_recv,
    drift_send,
    drift_recv,
):
    chans, height, width = x_ref.shape
    feats = lift_ref.shape[1]
    block = 3 * feats
    depth = 3 * block
    chunk = 64 if feats % 64 == 0 else feats
    tm = lax.axis_index("tm")
    space = lax.axis_index("space")
    has_up = space > 0
    has_down = space < tiles - 1

    pairs = (
        (x_hbm, x_ref),
        (embed_hbm, embed_ref),
        (lift_hbm, lift_ref),
        (project_hbm, project_ref),
        (conv_one_hbm, raw_one),
        (conv_two_hbm, raw_two),
    )
    loads = [pltpu.make_async_copy(a, b, load_sem.at[i]) for i, (a, b) in enumerate(pairs)]
    for load in loads:
        load.start()

    barrier = pltpu.get_barrier_semaphore()
    for shift in range(1, steps):
        other = lax.rem(tm + shift, steps)
        pl.semaphore_signal(barrier, inc=1, device_id=(other, space), device_id_type=MESH)

    @pl.when(has_up)
    def _():
        pl.semaphore_signal(barrier, inc=1, device_id=(tm, space - 1), device_id_type=MESH)

    @pl.when(has_down)
    def _():
        pl.semaphore_signal(barrier, inc=1, device_id=(tm, space + 1), device_id_type=MESH)

    def halo_copies(sweep):
        up = pltpu.make_async_remote_copy(
            src_ref=xb_rows.at[sweep, pl.ds(2, 2)],
            dst_ref=xb_rows.at[sweep, pl.ds(height + 2, 2)],
            send_sem=halo_send.at[sweep, 0],
            recv_sem=halo_recv.at[sweep, 1],
            device_id=(tm, space - 1),
            device_id_type=MESH,
        )
        down = pltpu.make_async_remote_copy(
            src_ref=xb_rows.at[sweep, pl.ds(height, 2)],
            dst_ref=xb_rows.at[sweep, pl.ds(0, 2)],
            send_sem=halo_send.at[sweep, 1],
            recv_sem=halo_recv.at[sweep, 0],
            device_id=(tm, space + 1),
            device_id_type=MESH,
        )
        return up, down

    def send_halo(sweep):
        up, down = halo_copies(sweep)

        @pl.when(has_up)
        def _():
            up.start()

        @pl.when(has_down)
        def _():
            down.start()

    def wait_halo(sweep):
        up, down = halo_copies(sweep)

        @pl.when(has_up)
        def _():
            down.wait_recv()

        @pl.when(has_down)
        def _():
            up.wait_recv()

    def drift_copy(sweep, shift, row):
        return pltpu.make_async_remote_copy(
            src_ref=drift_out.at[sweep, row],
            dst_ref=drift_in.at[sweep, shift - 1, row],
            send_sem=drift_send.at[sweep, shift - 1, row],
            recv_sem=drift_recv.at[sweep, shift - 1, row],
            device_id=(tm + shift, space),
            device_id_type=MESH,
        )

    def send_drift(sweep, row):
        for shift in range(1, steps):

            @pl.when(tm + shift < steps)
            def _():
                drift_copy(sweep, shift, row).start()

    def earlier(sweep, row):
        total = jnp.zeros((chans, width), jnp.float32)
        for shift in range(1, steps):

            @pl.when(tm >= shift)
            def _():
                drift_copy(sweep, shift, row).wait_recv()

            total = total + jnp.where(tm >= shift, drift_in[sweep, shift - 1, row], 0.0)
        return total

    lane = lax.broadcasted_iota(jnp.int32, (chunk, width), 1)
    zero = jnp.zeros((), jnp.bfloat16)

    def store_columns(cols, index, start, act):
        base = index * block + start
        mid = act.astype(jnp.bfloat16)
        left = jnp.where(lane == 0, zero, pltpu.roll(mid, 1, 1))
        right = jnp.where(lane == width - 1, zero, pltpu.roll(mid, width - 1, 1))
        cols[base : base + chunk, :] = left
        cols[base + feats : base + feats + chunk, :] = mid
        cols[base + 2 * feats : base + 2 * feats + chunk, :] = right

    def build(sweep, index):
        inside = None
        if index < 2:
            inside = has_up
        if index >= height + 2:
            inside = has_down
        xb = xb_rows[sweep, index]
        for start in range(0, feats, chunk):
            lifted = jnp.dot(
                lift_rows[start : start + chunk, :chans], xb, preferred_element_type=jnp.float32
            )
            lifted = lifted + jnp.concatenate(
                [embed_bc[start : start + chunk, :]] * (width // 128), axis=1
            )
            if 1 <= index <= height + 2:
                first[index - 1, start : start + chunk, :] = lifted
            act = silu(lifted)
            if inside is not None:
                act = jnp.where(inside, act, 0.0)
            store_columns(cols_one, index, start, act)

    def conv(weight, cols, index):
        return jnp.dot(
            weight[...],
            cols[index * block : index * block + depth, :],
            preferred_element_type=jnp.float32,
        )

    def activate_one(index):
        inside = None
        if index == 0:
            inside = has_up
        if index == height + 1:
            inside = has_down
        for start in range(0, feats, chunk):
            act = silu(sums_one[index % 2, start : start + chunk, :])
            if inside is not None:
                act = jnp.where(inside, act, 0.0)
            store_columns(cols_two, index, start, act)

    def finish_row(sweep, row):
        for start in range(0, feats, chunk):
            act = silu(sums_two[row % 2, start : start + chunk, :])
            act_three[row % 2, start : start + chunk, :] = act.astype(jnp.bfloat16)
        out = jnp.dot(project_ref[...], act_three[row % 2], preferred_element_type=jnp.float32)
        drift_out[sweep, row] = scale_ref[0] * out - decay_ref[0] * state_rows[row]

    def build_weight(raw, weight):
        for tap in range(9):
            weight[:, tap * feats : (tap + 1) * feats] = raw[tap // 3, tap % 3]

    def take_state(sweep, row):
        state = rows_f32[row] + earlier(sweep - 1, row)
        state_rows[row] = state
        xb_rows[sweep, row + 2] = state.astype(jnp.bfloat16)

    def one_sweep(sweep):
        edges = (0, 1, height - 1, height - 2)

        @pl.when(sweep > 0)
        def _():
            for row in edges:
                take_state(sweep, row)
            send_halo(sweep)
            take_state(sweep, 2)

        for index in (2, 3, 4):
            build(sweep, index)

        @pl.when(sweep == 0)
        def _():
            loads[4].wait()
            build_weight(raw_one, w_one)

        order = list(range(2, height)) + [1, height, 0, height + 1]
        builds = list(range(5, height + 2)) + [1, height + 2, 0, height + 3]
        before = None
        for turn, index in enumerate(order):
            fresh = builds[turn] if turn < len(builds) else None
            if fresh is not None and 5 <= fresh < height:

                @pl.when(sweep > 0)
                def _():
                    take_state(sweep, fresh - 2)

            if fresh == 1:
                wait_halo(sweep)
            value = first[index] + conv(w_one, cols_one, index)
            if fresh is not None:
                build(sweep, fresh)
            if before is not None:
                activate_one(before)
            first[index] = value
            sums_one[index % 2] = value
            before = index

        @pl.when(sweep == 0)
        def _():
            loads[5].wait()
            build_weight(raw_two, w_two)

        done = None
        for row in edges + tuple(range(2, height - 2)):
            value = first[row + 1] + conv(w_two, cols_two, row)
            if done is None:
                activate_one(before)
            else:
                finish_row(sweep, done)
            sums_two[row % 2] = value
            if done is not None:
                send_drift(sweep, done)
            done = row
        finish_row(sweep, done)
        send_drift(sweep, done)

    loads[0].wait()
    for row in range(height):
        value = x_ref[:, row, :]
        rows_f32[row] = value
        state_rows[row] = value
        xb_rows[0, row + 2] = value.astype(jnp.bfloat16)
    greeted = (steps - 1) + jnp.where(has_up, 1, 0) + jnp.where(has_down, 1, 0)
    pl.semaphore_wait(barrier, greeted)
    send_halo(0)
    for load in loads[1:4]:
        load.wait()
    wide = (-feats) % 128
    embed_bc[...] = jnp.transpose(
        jnp.pad(jnp.broadcast_to(embed_ref[...], (128, feats)), ((0, 0), (0, wide)))
    )[:feats]
    turned = jnp.transpose(
        jnp.pad(lift_ref[...].astype(jnp.float32), ((0, 128 - chans), (0, wide)))
    )[:feats]
    lift_rows[...] = turned.astype(jnp.bfloat16)

    @pl.loop(0, ITERS)
    def _(sweep):
        one_sweep(sweep)

    for row in range(height):
        total = drift_out[ITERS - 1, row] + earlier(ITERS - 1, row)
        out_ref[0, :, row, :] = rows_f32[row] + total

    for sweep in range(ITERS):
        up, down = halo_copies(sweep)

        @pl.when(has_up)
        def _():
            up.wait_send()

        @pl.when(has_down)
        def _():
            down.wait_send()

        for shift in range(1, steps):
            for row in range(height):

                @pl.when(tm + shift < steps)
                def _():
                    drift_copy(sweep, shift, row).wait_send()


def solution(mesh):
    steps, tiles = mesh.shape["tm"], mesh.shape["space"]

    def per_device(
        first_state,
        time_embed,
        drift_scale,
        state_decay,
        lift_weight,
        conv_one,
        conv_two,
        project_weight,
    ):
        chans, height, width = first_state.shape
        feats = lift_weight.shape[0]
        block, depth = 3 * feats, 9 * feats
        peers = max(steps - 1, 1)
        vmem = pl.BlockSpec(memory_space=pltpu.VMEM)
        smem = pl.BlockSpec(memory_space=pltpu.SMEM)
        hbm = pl.BlockSpec(memory_space=pl.ANY)
        return pl.pallas_call(
            functools.partial(kernel, steps, tiles),
            out_shape=jax.ShapeDtypeStruct((1, chans, height, width), jnp.float32),
            in_specs=[hbm, hbm, smem, smem, hbm, hbm, hbm, hbm],
            out_specs=vmem,
            scratch_shapes=[
                pltpu.VMEM((chans, height, width), jnp.float32),
                pltpu.VMEM((1, feats), jnp.float32),
                pltpu.VMEM((chans, feats), jnp.bfloat16),
                pltpu.VMEM((chans, feats), jnp.bfloat16),
                pltpu.VMEM((3, 3, feats, feats), jnp.bfloat16),
                pltpu.VMEM((3, 3, feats, feats), jnp.bfloat16),
                pltpu.VMEM((feats, depth), jnp.bfloat16),
                pltpu.VMEM((feats, depth), jnp.bfloat16),
                pltpu.VMEM((feats, 128), jnp.float32),
                pltpu.VMEM((feats, 128), jnp.bfloat16),
                pltpu.VMEM(((height + 4) * block, width), jnp.bfloat16),
                pltpu.VMEM(((height + 2) * block, width), jnp.bfloat16),
                pltpu.VMEM((height + 2, feats, width), jnp.float32),
                pltpu.VMEM((2, feats, width), jnp.float32),
                pltpu.VMEM((2, feats, width), jnp.float32),
                pltpu.VMEM((2, feats, width), jnp.bfloat16),
                pltpu.VMEM((height, chans, width), jnp.float32),
                pltpu.VMEM((height, chans, width), jnp.float32),
                pltpu.VMEM((ITERS, height + 4, chans, width), jnp.bfloat16),
                pltpu.VMEM((ITERS, height, chans, width), jnp.float32),
                pltpu.VMEM((ITERS, peers, height, chans, width), jnp.float32),
                pltpu.SemaphoreType.DMA((6,)),
                pltpu.SemaphoreType.DMA((ITERS, 2)),
                pltpu.SemaphoreType.DMA((ITERS, 2)),
                pltpu.SemaphoreType.DMA((ITERS, peers, height)),
                pltpu.SemaphoreType.DMA((ITERS, peers, height)),
            ],
            compiler_params=pltpu.CompilerParams(
                collective_id=0, has_side_effects=True, vmem_limit_bytes=67043328
            ),
        )(
            first_state,
            time_embed,
            drift_scale,
            state_decay,
            lift_weight.T,
            project_weight,
            conv_one,
            conv_two,
        )

    in_specs = (P(None, "space", None), P("tm", None), P("tm"), P("tm"), P(), P(), P(), P())
    return jax.shard_map(
        per_device,
        mesh=mesh,
        in_specs=in_specs,
        out_specs=P("tm", None, "space", None),
        check_vma=False,
    )
```

```python
import functools

import jax
import jax.numpy as jnp
from jax import lax
from jax.experimental import pallas as pl
from jax.experimental.pallas import tpu as pltpu
from jax.sharding import PartitionSpec as P

ITERS = 2
MESH = pl.DeviceIdType.MESH


def silu(v):
    half = 0.5 * v
    return half + half * jnp.tanh(half)


def kernel(
    steps,
    tiles,
    x_hbm,
    embed_hbm,
    scale_ref,
    decay_ref,
    lift_hbm,
    project_hbm,
    conv_one_hbm,
    conv_two_hbm,
    out_ref,
    x_ref,
    embed_ref,
    lift_ref,
    project_ref,
    raw_one,
    raw_two,
    w_one,
    w_two,
    embed_bc,
    lift_rows,
    cols_one,
    cols_two,
    first,
    sums_one,
    sums_two,
    act_three,
    rows_f32,
    state_rows,
    xb_rows,
    drift_out,
    drift_in,
    load_sem,
    halo_send,
    halo_recv,
    drift_send,
    drift_recv,
):
    chans, height, width = x_ref.shape
    feats = lift_ref.shape[1]
    block = 3 * feats
    depth = 3 * block
    chunk = 64 if feats % 64 == 0 else feats
    tm = lax.axis_index("tm")
    space = lax.axis_index("space")
    has_up = space > 0
    has_down = space < tiles - 1

    pairs = (
        (x_hbm, x_ref),
        (embed_hbm, embed_ref),
        (lift_hbm, lift_ref),
        (project_hbm, project_ref),
        (conv_one_hbm, raw_one),
        (conv_two_hbm, raw_two),
    )
    loads = [pltpu.make_async_copy(a, b, load_sem.at[i]) for i, (a, b) in enumerate(pairs)]
    for load in loads:
        load.start()

    barrier = pltpu.get_barrier_semaphore()
    for shift in range(1, steps):
        other = lax.rem(tm + shift, steps)
        pl.semaphore_signal(barrier, inc=1, device_id=(other, space), device_id_type=MESH)

    @pl.when(has_up)
    def _():
        pl.semaphore_signal(barrier, inc=1, device_id=(tm, space - 1), device_id_type=MESH)

    @pl.when(has_down)
    def _():
        pl.semaphore_signal(barrier, inc=1, device_id=(tm, space + 1), device_id_type=MESH)

    def halo_copies(sweep):
        up = pltpu.make_async_remote_copy(
            src_ref=xb_rows.at[sweep, pl.ds(2, 2)],
            dst_ref=xb_rows.at[sweep, pl.ds(height + 2, 2)],
            send_sem=halo_send.at[sweep, 0],
            recv_sem=halo_recv.at[sweep, 1],
            device_id=(tm, space - 1),
            device_id_type=MESH,
        )
        down = pltpu.make_async_remote_copy(
            src_ref=xb_rows.at[sweep, pl.ds(height, 2)],
            dst_ref=xb_rows.at[sweep, pl.ds(0, 2)],
            send_sem=halo_send.at[sweep, 1],
            recv_sem=halo_recv.at[sweep, 0],
            device_id=(tm, space + 1),
            device_id_type=MESH,
        )
        return up, down

    def send_halo(sweep):
        up, down = halo_copies(sweep)

        @pl.when(has_up)
        def _():
            up.start()

        @pl.when(has_down)
        def _():
            down.start()

    def wait_halo(sweep):
        up, down = halo_copies(sweep)

        @pl.when(has_up)
        def _():
            down.wait_recv()

        @pl.when(has_down)
        def _():
            up.wait_recv()

    def drift_copy(sweep, shift, row):
        return pltpu.make_async_remote_copy(
            src_ref=drift_out.at[sweep, row],
            dst_ref=drift_in.at[sweep, shift - 1, row],
            send_sem=drift_send.at[sweep, shift - 1, row],
            recv_sem=drift_recv.at[sweep, shift - 1, row],
            device_id=(tm + shift, space),
            device_id_type=MESH,
        )

    def send_drift(sweep, row):
        for shift in range(1, steps):

            @pl.when(tm + shift < steps)
            def _():
                drift_copy(sweep, shift, row).start()

    def earlier(sweep, row):
        total = jnp.zeros((chans, width), jnp.float32)
        for shift in range(1, steps):

            @pl.when(tm >= shift)
            def _():
                drift_copy(sweep, shift, row).wait_recv()

            total = total + jnp.where(tm >= shift, drift_in[sweep, shift - 1, row], 0.0)
        return total

    lane = lax.broadcasted_iota(jnp.int32, (chunk, width), 1)
    zero = jnp.zeros((), jnp.bfloat16)

    def store_columns(cols, index, start, act):
        base = index * block + start
        mid = act.astype(jnp.bfloat16)
        left = jnp.where(lane == 0, zero, pltpu.roll(mid, 1, 1))
        right = jnp.where(lane == width - 1, zero, pltpu.roll(mid, width - 1, 1))
        cols[base : base + chunk, :] = left
        cols[base + feats : base + feats + chunk, :] = mid
        cols[base + 2 * feats : base + 2 * feats + chunk, :] = right

    def build(sweep, index):
        inside = None
        if index < 2:
            inside = has_up
        if index >= height + 2:
            inside = has_down
        xb = xb_rows[sweep, index]
        for start in range(0, feats, chunk):
            lifted = jnp.dot(
                lift_rows[start : start + chunk, :chans], xb, preferred_element_type=jnp.float32
            )
            lifted = lifted + jnp.concatenate(
                [embed_bc[start : start + chunk, :]] * (width // 128), axis=1
            )
            if 1 <= index <= height + 2:
                first[index - 1, start : start + chunk, :] = lifted
            act = silu(lifted)
            if inside is not None:
                act = jnp.where(inside, act, 0.0)
            store_columns(cols_one, index, start, act)

    def conv_pair(weight, cols, pair):
        taken = [cols[index * block : index * block + depth, :] for index in pair]
        return jnp.dot(
            weight[...], jnp.concatenate(taken, axis=1), preferred_element_type=jnp.float32
        )

    def activate_one(index, slot):
        inside = None
        if index == 0:
            inside = has_up
        if index == height + 1:
            inside = has_down
        for start in range(0, feats, chunk):
            act = silu(sums_one[slot, start : start + chunk, :])
            if inside is not None:
                act = jnp.where(inside, act, 0.0)
            store_columns(cols_two, index, start, act)

    def finish_pair(sweep, pair, slot):
        for start in range(0, feats, chunk):
            for half in range(2):
                act = silu(sums_two[slot + half, start : start + chunk, :])
                act_three[
                    slot // 2, start : start + chunk, half * width : (half + 1) * width
                ] = act.astype(jnp.bfloat16)
        out = jnp.dot(project_ref[...], act_three[slot // 2], preferred_element_type=jnp.float32)
        for half, row in enumerate(pair):
            part = out[:, half * width : (half + 1) * width]
            drift_out[sweep, row] = scale_ref[0] * part - decay_ref[0] * state_rows[row]

    def build_weight(raw, weight):
        for tap in range(9):
            weight[:, tap * feats : (tap + 1) * feats] = raw[tap // 3, tap % 3]

    def take_state(sweep, row):
        state = rows_f32[row] + earlier(sweep - 1, row)
        state_rows[row] = state
        xb_rows[sweep, row + 2] = state.astype(jnp.bfloat16)

    def one_sweep(sweep):
        edges = (0, 1, height - 1, height - 2)
        middle = tuple(range(2, height - 2))

        @pl.when(sweep > 0)
        def _():
            for row in edges:
                take_state(sweep, row)
            send_halo(sweep)
            take_state(sweep, 2)
            take_state(sweep, 3)

        for index in (2, 3, 4, 5):
            build(sweep, index)

        @pl.when(sweep == 0)
        def _():
            loads[4].wait()
            build_weight(raw_one, w_one)

        order = [(index, index + 1) for index in range(2, height, 2)]
        order += [(1, height), (0, height + 1)]
        builds = [(index + 4, index + 5) for index in range(2, height - 2, 2)]
        builds += [(1, height + 2), (0, height + 3), ()]
        before = None
        for turn, pair in enumerate(order):
            fresh = builds[turn]
            late = [index - 2 for index in fresh if 6 <= index < height]
            if late:

                @pl.when(sweep > 0)
                def _():
                    for row in late:
                        take_state(sweep, row)

            if 1 in fresh:
                wait_halo(sweep)
            value = conv_pair(w_one, cols_one, pair)
            for index in fresh:
                build(sweep, index)
            slot = 2 * (turn % 2)
            if before is not None:
                for half, index in enumerate(before):
                    activate_one(index, 2 - slot + half)
            for half, index in enumerate(pair):
                part = first[index] + value[:, half * width : (half + 1) * width]
                first[index] = part
                sums_one[slot + half] = part
            before, last = pair, slot

        @pl.when(sweep == 0)
        def _():
            loads[5].wait()
            build_weight(raw_two, w_two)

        pairs = [edges[:2], edges[2:]]
        pairs += [middle[place : place + 2] for place in range(0, len(middle), 2)]
        for half, index in enumerate(before):
            activate_one(index, last + half)
        done = None
        for turn, pair in enumerate(pairs):
            value = conv_pair(w_two, cols_two, pair)
            slot = 2 * (turn % 2)
            if done is not None:
                finish_pair(sweep, done, 2 - slot)
            for half, row in enumerate(pair):
                sums_two[slot + half] = (
                    first[row + 1] + value[:, half * width : (half + 1) * width]
                )
            if done is not None:
                for row in done:
                    send_drift(sweep, row)
            done = pair
        finish_pair(sweep, done, slot)
        for row in done:
            send_drift(sweep, row)

    loads[0].wait()
    for row in range(height):
        value = x_ref[:, row, :]
        rows_f32[row] = value
        state_rows[row] = value
        xb_rows[0, row + 2] = value.astype(jnp.bfloat16)
    greeted = (steps - 1) + jnp.where(has_up, 1, 0) + jnp.where(has_down, 1, 0)
    pl.semaphore_wait(barrier, greeted)
    send_halo(0)
    for load in loads[1:4]:
        load.wait()
    wide = (-feats) % 128
    embed_bc[...] = jnp.transpose(
        jnp.pad(jnp.broadcast_to(embed_ref[...], (128, feats)), ((0, 0), (0, wide)))
    )[:feats]
    turned = jnp.transpose(
        jnp.pad(lift_ref[...].astype(jnp.float32), ((0, 128 - chans), (0, wide)))
    )[:feats]
    lift_rows[...] = turned.astype(jnp.bfloat16)

    @pl.loop(0, ITERS)
    def _(sweep):
        one_sweep(sweep)

    for row in range(height):
        total = drift_out[ITERS - 1, row] + earlier(ITERS - 1, row)
        out_ref[0, :, row, :] = rows_f32[row] + total

    for sweep in range(ITERS):
        up, down = halo_copies(sweep)

        @pl.when(has_up)
        def _():
            up.wait_send()

        @pl.when(has_down)
        def _():
            down.wait_send()

        for shift in range(1, steps):
            for row in range(height):

                @pl.when(tm + shift < steps)
                def _():
                    drift_copy(sweep, shift, row).wait_send()


def solution(mesh):
    steps, tiles = mesh.shape["tm"], mesh.shape["space"]

    def per_device(
        first_state,
        time_embed,
        drift_scale,
        state_decay,
        lift_weight,
        conv_one,
        conv_two,
        project_weight,
    ):
        chans, height, width = first_state.shape
        feats = lift_weight.shape[0]
        block, depth = 3 * feats, 9 * feats
        peers = max(steps - 1, 1)
        vmem = pl.BlockSpec(memory_space=pltpu.VMEM)
        smem = pl.BlockSpec(memory_space=pltpu.SMEM)
        hbm = pl.BlockSpec(memory_space=pl.ANY)
        return pl.pallas_call(
            functools.partial(kernel, steps, tiles),
            out_shape=jax.ShapeDtypeStruct((1, chans, height, width), jnp.float32),
            in_specs=[hbm, hbm, smem, smem, hbm, hbm, hbm, hbm],
            out_specs=vmem,
            scratch_shapes=[
                pltpu.VMEM((chans, height, width), jnp.float32),
                pltpu.VMEM((1, feats), jnp.float32),
                pltpu.VMEM((chans, feats), jnp.bfloat16),
                pltpu.VMEM((chans, feats), jnp.bfloat16),
                pltpu.VMEM((3, 3, feats, feats), jnp.bfloat16),
                pltpu.VMEM((3, 3, feats, feats), jnp.bfloat16),
                pltpu.VMEM((feats, depth), jnp.bfloat16),
                pltpu.VMEM((feats, depth), jnp.bfloat16),
                pltpu.VMEM((feats, 128), jnp.float32),
                pltpu.VMEM((feats, 128), jnp.bfloat16),
                pltpu.VMEM(((height + 4) * block, width), jnp.bfloat16),
                pltpu.VMEM(((height + 2) * block, width), jnp.bfloat16),
                pltpu.VMEM((height + 2, feats, width), jnp.float32),
                pltpu.VMEM((4, feats, width), jnp.float32),
                pltpu.VMEM((4, feats, width), jnp.float32),
                pltpu.VMEM((2, feats, 2 * width), jnp.bfloat16),
                pltpu.VMEM((height, chans, width), jnp.float32),
                pltpu.VMEM((height, chans, width), jnp.float32),
                pltpu.VMEM((ITERS, height + 4, chans, width), jnp.bfloat16),
                pltpu.VMEM((ITERS, height, chans, width), jnp.float32),
                pltpu.VMEM((ITERS, peers, height, chans, width), jnp.float32),
                pltpu.SemaphoreType.DMA((6,)),
                pltpu.SemaphoreType.DMA((ITERS, 2)),
                pltpu.SemaphoreType.DMA((ITERS, 2)),
                pltpu.SemaphoreType.DMA((ITERS, peers, height)),
                pltpu.SemaphoreType.DMA((ITERS, peers, height)),
            ],
            compiler_params=pltpu.CompilerParams(
                collective_id=0, has_side_effects=True, vmem_limit_bytes=67043328
            ),
        )(
            first_state,
            time_embed,
            drift_scale,
            state_decay,
            lift_weight.T,
            project_weight,
            conv_one,
            conv_two,
        )

    in_specs = (P(None, "space", None), P("tm", None), P("tm"), P("tm"), P(), P(), P(), P())
    return jax.shard_map(
        per_device,
        mesh=mesh,
        in_specs=in_specs,
        out_specs=P("tm", None, "space", None),
        check_vma=False,
    )
```

```python
import functools

import jax
import jax.numpy as jnp
from jax import lax
from jax.experimental import pallas as pl
from jax.experimental.pallas import tpu as pltpu
from jax.sharding import PartitionSpec as P

ITERS = 2
MESH = pl.DeviceIdType.MESH


def silu(v):
    half = 0.5 * v
    return half + half * jnp.tanh(half)


def kernel(
    steps,
    tiles,
    x_hbm,
    embed_hbm,
    scale_ref,
    decay_ref,
    lift_hbm,
    project_hbm,
    conv_one_hbm,
    conv_two_hbm,
    out_ref,
    x_ref,
    embed_ref,
    lift_ref,
    project_ref,
    raw_one,
    raw_two,
    w_one,
    w_two,
    embed_bc,
    lift_rows,
    cols_one,
    cols_two,
    first,
    sums_one,
    sums_two,
    act_three,
    rows_f32,
    state_rows,
    xb_rows,
    drift_out,
    drift_in,
    load_sem,
    halo_send,
    halo_recv,
    drift_send,
    drift_recv,
):
    chans, height, width = x_ref.shape
    feats = lift_ref.shape[1]
    block = 3 * feats
    depth = 3 * block
    chunk = 64 if feats % 64 == 0 else feats
    tm = lax.axis_index("tm")
    space = lax.axis_index("space")
    has_up = space > 0
    has_down = space < tiles - 1

    pairs = (
        (x_hbm, x_ref),
        (embed_hbm, embed_ref),
        (lift_hbm, lift_ref),
        (project_hbm, project_ref),
        (conv_one_hbm, raw_one),
        (conv_two_hbm, raw_two),
    )
    loads = [pltpu.make_async_copy(a, b, load_sem.at[i]) for i, (a, b) in enumerate(pairs)]
    for load in loads:
        load.start()

    barrier = pltpu.get_barrier_semaphore()
    for shift in range(1, steps):
        other = lax.rem(tm + shift, steps)
        pl.semaphore_signal(barrier, inc=1, device_id=(other, space), device_id_type=MESH)

    @pl.when(has_up)
    def _():
        pl.semaphore_signal(barrier, inc=1, device_id=(tm, space - 1), device_id_type=MESH)

    @pl.when(has_down)
    def _():
        pl.semaphore_signal(barrier, inc=1, device_id=(tm, space + 1), device_id_type=MESH)

    def halo_copies(sweep):
        up = pltpu.make_async_remote_copy(
            src_ref=xb_rows.at[sweep, pl.ds(2, 2)],
            dst_ref=xb_rows.at[sweep, pl.ds(height + 2, 2)],
            send_sem=halo_send.at[sweep, 0],
            recv_sem=halo_recv.at[sweep, 1],
            device_id=(tm, space - 1),
            device_id_type=MESH,
        )
        down = pltpu.make_async_remote_copy(
            src_ref=xb_rows.at[sweep, pl.ds(height, 2)],
            dst_ref=xb_rows.at[sweep, pl.ds(0, 2)],
            send_sem=halo_send.at[sweep, 1],
            recv_sem=halo_recv.at[sweep, 0],
            device_id=(tm, space + 1),
            device_id_type=MESH,
        )
        return up, down

    def send_halo(sweep):
        up, down = halo_copies(sweep)

        @pl.when(has_up)
        def _():
            up.start()

        @pl.when(has_down)
        def _():
            down.start()

    def wait_halo(sweep):
        up, down = halo_copies(sweep)

        @pl.when(has_up)
        def _():
            down.wait_recv()

        @pl.when(has_down)
        def _():
            up.wait_recv()

    def drift_copy(sweep, shift, row):
        return pltpu.make_async_remote_copy(
            src_ref=drift_out.at[sweep, row],
            dst_ref=drift_in.at[sweep, shift - 1, row],
            send_sem=drift_send.at[sweep, shift - 1, row],
            recv_sem=drift_recv.at[sweep, shift - 1, row],
            device_id=(tm + shift, space),
            device_id_type=MESH,
        )

    def send_drift(sweep, row):
        for shift in range(1, steps):

            @pl.when(tm + shift < steps)
            def _():
                drift_copy(sweep, shift, row).start()

    def earlier(sweep, row):
        total = jnp.zeros((chans, width), jnp.float32)
        for shift in range(1, steps):

            @pl.when(tm >= shift)
            def _():
                drift_copy(sweep, shift, row).wait_recv()

            total = total + jnp.where(tm >= shift, drift_in[sweep, shift - 1, row], 0.0)
        return total

    lane = lax.broadcasted_iota(jnp.int32, (chunk, width), 1)
    zero = jnp.zeros((), jnp.bfloat16)

    def store_columns(cols, index, start, act):
        base = index * block + start
        mid = act.astype(jnp.bfloat16)
        left = jnp.where(lane == 0, zero, pltpu.roll(mid, 1, 1))
        right = jnp.where(lane == width - 1, zero, pltpu.roll(mid, width - 1, 1))
        cols[base : base + chunk, :] = left
        cols[base + feats : base + feats + chunk, :] = mid
        cols[base + 2 * feats : base + 2 * feats + chunk, :] = right

    def lift(sweep, pair):
        xb = jnp.concatenate([xb_rows[sweep, index] for index in pair], axis=1)
        value = jnp.dot(lift_rows[:, :chans], xb, preferred_element_type=jnp.float32)
        embed = jnp.concatenate([embed_bc[...]] * (width // 128), axis=1)
        for half, index in enumerate(pair):
            first[index] = value[:, half * width : (half + 1) * width] + embed

    def build(index):
        inside = None
        if index < 2:
            inside = has_up
        if index >= height + 2:
            inside = has_down
        for start in range(0, feats, chunk):
            act = silu(first[index, start : start + chunk, :])
            if inside is not None:
                act = jnp.where(inside, act, 0.0)
            store_columns(cols_one, index, start, act)

    def conv_pair(weight, cols, pair):
        taken = [cols[index * block : index * block + depth, :] for index in pair]
        return jnp.dot(
            weight[...], jnp.concatenate(taken, axis=1), preferred_element_type=jnp.float32
        )

    def activate_one(index, slot):
        inside = None
        if index == 0:
            inside = has_up
        if index == height + 1:
            inside = has_down
        for start in range(0, feats, chunk):
            act = silu(sums_one[slot, start : start + chunk, :])
            if inside is not None:
                act = jnp.where(inside, act, 0.0)
            store_columns(cols_two, index, start, act)

    def finish_pair(sweep, pair, slot):
        for start in range(0, feats, chunk):
            for half in range(2):
                act = silu(sums_two[slot + half, start : start + chunk, :])
                act_three[
                    slot // 2, start : start + chunk, half * width : (half + 1) * width
                ] = act.astype(jnp.bfloat16)
        out = jnp.dot(project_ref[...], act_three[slot // 2], preferred_element_type=jnp.float32)
        for half, row in enumerate(pair):
            part = out[:, half * width : (half + 1) * width]
            drift_out[sweep, row] = scale_ref[0] * part - decay_ref[0] * state_rows[row]

    def build_weight(raw, weight, taps=range(9)):
        for tap in taps:
            weight[:, tap * feats : (tap + 1) * feats] = raw[tap // 3, tap % 3]

    def take_state(sweep, row):
        state = rows_f32[row] + earlier(sweep - 1, row)
        state_rows[row] = state
        xb_rows[sweep, row + 2] = state.astype(jnp.bfloat16)

    def one_sweep(sweep):
        edges = (0, 1, height - 1, height - 2)
        middle = tuple(range(2, height - 2))

        @pl.when(sweep > 0)
        def _():
            for row in range(4):
                take_state(sweep, row)

        for pair in ((2, 3), (4, 5)):
            lift(sweep, pair)
        for index in (2, 3, 4, 5):
            build(index)

        @pl.when(sweep == 0)
        def _():
            loads[4].wait()
            build_weight(raw_one, w_one)

        order = [(index, index + 1) for index in range(2, height, 2)]
        order += [(1, height), (0, height + 1)]
        builds = [(index + 4, index + 5) for index in range(2, height - 2, 2)]
        builds += [(1, height + 2), (0, height + 3), ()]
        before = None
        for turn, pair in enumerate(order):
            fresh = builds[turn]
            if turn == 0:

                @pl.when(sweep > 0)
                def _():
                    for row in range(height - 1, 3, -1):
                        take_state(sweep, row)
                    send_halo(sweep)

            if 1 in fresh:
                wait_halo(sweep)
            if fresh:
                lift(sweep, fresh)
            if turn == len(order) - 2:

                @pl.when(sweep == 0)
                def _():
                    loads[5].wait()

            value = conv_pair(w_one, cols_one, pair)
            if turn == len(order) - 2:
                build_weight(raw_two, w_two, range(2))
            if turn == len(order) - 1:
                build_weight(raw_two, w_two, range(2, 9))
            for index in fresh:
                build(index)
            slot = 2 * (turn % 2)
            if before is not None:
                for half, index in enumerate(before):
                    activate_one(index, 2 - slot + half)
            for half, index in enumerate(pair):
                part = first[index + 1] + value[:, half * width : (half + 1) * width]
                first[index + 1] = part
                sums_one[slot + half] = part
            before, last = pair, slot

        pairs = [middle[:2], edges[:2], edges[2:]]
        pairs += [middle[place : place + 2] for place in range(2, len(middle), 2)]
        done = None
        for turn, pair in enumerate(pairs):
            value = conv_pair(w_two, cols_two, pair)
            slot = 2 * (turn % 2)
            if done is None:
                for half, index in enumerate(before):
                    activate_one(index, last + half)
            else:
                finish_pair(sweep, done, 2 - slot)
            for half, row in enumerate(pair):
                sums_two[slot + half] = (
                    first[row + 2] + value[:, half * width : (half + 1) * width]
                )
            if done is not None:
                for row in done:
                    send_drift(sweep, row)
            done = pair
        finish_pair(sweep, done, slot)
        for row in done:
            send_drift(sweep, row)

    loads[0].wait()
    for row in range(height):
        value = x_ref[:, row, :]
        rows_f32[row] = value
        state_rows[row] = value
        xb_rows[0, row + 2] = value.astype(jnp.bfloat16)
    greeted = (steps - 1) + jnp.where(has_up, 1, 0) + jnp.where(has_down, 1, 0)
    pl.semaphore_wait(barrier, greeted)
    send_halo(0)
    for load in loads[1:4]:
        load.wait()
    wide = (-feats) % 128
    embed_bc[...] = jnp.transpose(
        jnp.pad(jnp.broadcast_to(embed_ref[...], (128, feats)), ((0, 0), (0, wide)))
    )[:feats]
    turned = jnp.transpose(
        jnp.pad(lift_ref[...].astype(jnp.float32), ((0, 128 - chans), (0, wide)))
    )[:feats]
    lift_rows[...] = turned.astype(jnp.bfloat16)

    @pl.loop(0, ITERS)
    def _(sweep):
        one_sweep(sweep)

    for row in range(height):
        total = drift_out[ITERS - 1, row] + earlier(ITERS - 1, row)
        out_ref[0, :, row, :] = rows_f32[row] + total

    for sweep in range(ITERS):
        up, down = halo_copies(sweep)

        @pl.when(has_up)
        def _():
            up.wait_send()

        @pl.when(has_down)
        def _():
            down.wait_send()

        for shift in range(1, steps):
            for row in range(height):

                @pl.when(tm + shift < steps)
                def _():
                    drift_copy(sweep, shift, row).wait_send()


def solution(mesh):
    steps, tiles = mesh.shape["tm"], mesh.shape["space"]

    def per_device(
        first_state,
        time_embed,
        drift_scale,
        state_decay,
        lift_weight,
        conv_one,
        conv_two,
        project_weight,
    ):
        chans, height, width = first_state.shape
        feats = lift_weight.shape[0]
        block, depth = 3 * feats, 9 * feats
        peers = max(steps - 1, 1)
        vmem = pl.BlockSpec(memory_space=pltpu.VMEM)
        smem = pl.BlockSpec(memory_space=pltpu.SMEM)
        hbm = pl.BlockSpec(memory_space=pltpu.HBM)
        return pl.pallas_call(
            functools.partial(kernel, steps, tiles),
            out_shape=jax.ShapeDtypeStruct((1, chans, height, width), jnp.float32),
            in_specs=[hbm, hbm, smem, smem, hbm, hbm, hbm, hbm],
            out_specs=vmem,
            scratch_shapes=[
                pltpu.VMEM((chans, height, width), jnp.float32),
                pltpu.VMEM((1, feats), jnp.float32),
                pltpu.VMEM((chans, feats), jnp.bfloat16),
                pltpu.VMEM((chans, feats), jnp.bfloat16),
                pltpu.VMEM((3, 3, feats, feats), jnp.bfloat16),
                pltpu.VMEM((3, 3, feats, feats), jnp.bfloat16),
                pltpu.VMEM((feats, depth), jnp.bfloat16),
                pltpu.VMEM((feats, depth), jnp.bfloat16),
                pltpu.VMEM((feats, 128), jnp.float32),
                pltpu.VMEM((feats, 128), jnp.bfloat16),
                pltpu.VMEM(((height + 4) * block, width), jnp.bfloat16),
                pltpu.VMEM(((height + 2) * block, width), jnp.bfloat16),
                pltpu.VMEM((height + 4, feats, width), jnp.float32),
                pltpu.VMEM((4, feats, width), jnp.float32),
                pltpu.VMEM((4, feats, width), jnp.float32),
                pltpu.VMEM((2, feats, 2 * width), jnp.bfloat16),
                pltpu.VMEM((height, chans, width), jnp.float32),
                pltpu.VMEM((height, chans, width), jnp.float32),
                pltpu.VMEM((ITERS, height + 4, chans, width), jnp.bfloat16),
                pltpu.VMEM((ITERS, height, chans, width), jnp.float32),
                pltpu.VMEM((ITERS, peers, height, chans, width), jnp.float32),
                pltpu.SemaphoreType.DMA((6,)),
                pltpu.SemaphoreType.DMA((ITERS, 2)),
                pltpu.SemaphoreType.DMA((ITERS, 2)),
                pltpu.SemaphoreType.DMA((ITERS, peers, height)),
                pltpu.SemaphoreType.DMA((ITERS, peers, height)),
            ],
            compiler_params=pltpu.CompilerParams(
                collective_id=0, has_side_effects=True, vmem_limit_bytes=67043328
            ),
        )(
            first_state,
            time_embed,
            drift_scale,
            state_decay,
            lift_weight.T,
            project_weight,
            conv_one,
            conv_two,
        )

    in_specs = (P(None, "space", None), P("tm", None), P("tm"), P("tm"), P(), P(), P(), P())
    return jax.shard_map(
        per_device,
        mesh=mesh,
        in_specs=in_specs,
        out_specs=P("tm", None, "space", None),
        check_vma=False,
    )
```

```python
import functools

import jax
import jax.numpy as jnp
from jax import lax
from jax.experimental import pallas as pl
from jax.experimental.pallas import tpu as pltpu
from jax.sharding import PartitionSpec as P

ITERS = 2
MESH = pl.DeviceIdType.MESH


def silu(v):
    half = 0.5 * v
    return half + half * jnp.tanh(half)


def kernel(
    steps,
    tiles,
    x_hbm,
    embed_hbm,
    scale_ref,
    decay_ref,
    lift_hbm,
    project_hbm,
    conv_one_hbm,
    conv_two_hbm,
    out_ref,
    x_ref,
    embed_ref,
    lift_ref,
    project_ref,
    raw_one,
    raw_two,
    w_one,
    w_two,
    embed_bc,
    lift_rows,
    cols_one,
    cols_two,
    first,
    sums_one,
    sums_two,
    act_three,
    rows_f32,
    state_rows,
    xb_rows,
    drift_out,
    drift_in,
    load_sem,
    halo_send,
    halo_recv,
    drift_send,
    drift_recv,
):
    chans, height, width = x_ref.shape
    feats = lift_ref.shape[1]
    block = 3 * feats
    depth = 3 * block
    chunk = 64 if feats % 64 == 0 else feats
    tm = lax.axis_index("tm")
    space = lax.axis_index("space")
    has_up = space > 0
    has_down = space < tiles - 1

    pairs = (
        (x_hbm, x_ref),
        (embed_hbm, embed_ref),
        (lift_hbm, lift_ref),
        (project_hbm, project_ref),
        (conv_one_hbm, raw_one),
        (conv_two_hbm, raw_two),
    )
    loads = [pltpu.make_async_copy(a, b, load_sem.at[i]) for i, (a, b) in enumerate(pairs)]
    for load in loads:
        load.start()

    barrier = pltpu.get_barrier_semaphore()
    for shift in range(1, steps):
        other = lax.rem(tm + shift, steps)
        pl.semaphore_signal(barrier, inc=1, device_id=(other, space), device_id_type=MESH)

    @pl.when(has_up)
    def _():
        pl.semaphore_signal(barrier, inc=1, device_id=(tm, space - 1), device_id_type=MESH)

    @pl.when(has_down)
    def _():
        pl.semaphore_signal(barrier, inc=1, device_id=(tm, space + 1), device_id_type=MESH)

    def halo_copies(sweep):
        up = pltpu.make_async_remote_copy(
            src_ref=xb_rows.at[sweep, pl.ds(2, 2)],
            dst_ref=xb_rows.at[sweep, pl.ds(height + 2, 2)],
            send_sem=halo_send.at[sweep, 0],
            recv_sem=halo_recv.at[sweep, 1],
            device_id=(tm, space - 1),
            device_id_type=MESH,
        )
        down = pltpu.make_async_remote_copy(
            src_ref=xb_rows.at[sweep, pl.ds(height, 2)],
            dst_ref=xb_rows.at[sweep, pl.ds(0, 2)],
            send_sem=halo_send.at[sweep, 1],
            recv_sem=halo_recv.at[sweep, 0],
            device_id=(tm, space + 1),
            device_id_type=MESH,
        )
        return up, down

    def send_halo(sweep):
        up, down = halo_copies(sweep)

        @pl.when(has_up)
        def _():
            up.start()

        @pl.when(has_down)
        def _():
            down.start()

    def wait_halo(sweep):
        up, down = halo_copies(sweep)

        @pl.when(has_up)
        def _():
            down.wait_recv()

        @pl.when(has_down)
        def _():
            up.wait_recv()

    def drift_copy(sweep, shift, pair):
        return pltpu.make_async_remote_copy(
            src_ref=drift_out.at[sweep, pl.ds(2 * pair, 2)],
            dst_ref=drift_in.at[sweep, shift - 1, pl.ds(2 * pair, 2)],
            send_sem=drift_send.at[sweep, shift - 1, pair],
            recv_sem=drift_recv.at[sweep, shift - 1, pair],
            device_id=(tm + shift, space),
            device_id_type=MESH,
        )

    def send_drift(sweep, pair):
        for shift in range(1, steps):

            @pl.when(tm + shift < steps)
            def _():
                drift_copy(sweep, shift, pair).start()

    def wait_drift(sweep, pair):
        for shift in range(1, steps):

            @pl.when(tm >= shift)
            def _():
                drift_copy(sweep, shift, pair).wait_recv()

    def earlier(sweep, row):
        total = jnp.zeros((chans, width), jnp.float32)
        for shift in range(1, steps):
            total = total + jnp.where(tm >= shift, drift_in[sweep, shift - 1, row], 0.0)
        return total

    lane = lax.broadcasted_iota(jnp.int32, (chunk, width), 1)
    zero = jnp.zeros((), jnp.bfloat16)

    def store_columns(cols, index, start, act):
        base = index * block + start
        mid = act.astype(jnp.bfloat16)
        left = jnp.where(lane == 0, zero, pltpu.roll(mid, 1, 1))
        right = jnp.where(lane == width - 1, zero, pltpu.roll(mid, width - 1, 1))
        cols[base : base + chunk, :] = left
        cols[base + feats : base + feats + chunk, :] = mid
        cols[base + 2 * feats : base + 2 * feats + chunk, :] = right

    def lift(sweep, pair):
        xb = jnp.concatenate([xb_rows[sweep, index] for index in pair], axis=1)
        value = jnp.dot(lift_rows[:, :chans], xb, preferred_element_type=jnp.float32)
        embed = jnp.concatenate([embed_bc[...]] * (width // 128), axis=1)
        for half, index in enumerate(pair):
            first[index] = value[:, half * width : (half + 1) * width] + embed

    def build(index):
        inside = None
        if index < 2:
            inside = has_up
        if index >= height + 2:
            inside = has_down
        for start in range(0, feats, chunk):
            act = silu(first[index, start : start + chunk, :])
            if inside is not None:
                act = jnp.where(inside, act, 0.0)
            store_columns(cols_one, index, start, act)

    def conv_pair(weight, cols, pair):
        taken = [cols[index * block : index * block + depth, :] for index in pair]
        return jnp.dot(
            weight[...], jnp.concatenate(taken, axis=1), preferred_element_type=jnp.float32
        )

    def activate_one(index, slot):
        inside = None
        if index == 0:
            inside = has_up
        if index == height + 1:
            inside = has_down
        for start in range(0, feats, chunk):
            act = silu(sums_one[slot, start : start + chunk, :])
            if inside is not None:
                act = jnp.where(inside, act, 0.0)
            store_columns(cols_two, index, start, act)

    def finish_pair(sweep, pair, slot):
        for start in range(0, feats, chunk):
            for half in range(2):
                act = silu(sums_two[slot + half, start : start + chunk, :])
                act_three[
                    slot // 2, start : start + chunk, half * width : (half + 1) * width
                ] = act.astype(jnp.bfloat16)
        out = jnp.dot(project_ref[...], act_three[slot // 2], preferred_element_type=jnp.float32)
        for half, row in enumerate(pair):
            part = out[:, half * width : (half + 1) * width]
            drift_out[sweep, row] = scale_ref[0] * part - decay_ref[0] * state_rows[row]

    def build_weight(raw, weight, taps=range(9)):
        for tap in taps:
            weight[:, tap * feats : (tap + 1) * feats] = raw[tap // 3, tap % 3]

    def take_states(sweep, pair):
        wait_drift(sweep - 1, pair)
        for row in (2 * pair, 2 * pair + 1):
            state = rows_f32[row] + earlier(sweep - 1, row)
            state_rows[row] = state
            xb_rows[sweep, row + 2] = state.astype(jnp.bfloat16)

    def one_sweep(sweep):
        edges = (0, 1, height - 2, height - 1)
        middle = tuple(range(2, height - 2))

        @pl.when(sweep > 0)
        def _():
            for pair in range(2):
                take_states(sweep, pair)

        for pair in ((2, 3), (4, 5)):
            lift(sweep, pair)
        for index in (2, 3, 4, 5):
            build(index)

        @pl.when(sweep == 0)
        def _():
            loads[4].wait()
            build_weight(raw_one, w_one)

        order = [(index, index + 1) for index in range(2, height, 2)]
        order += [(1, height), (0, height + 1)]
        builds = [(index + 4, index + 5) for index in range(2, height - 2, 2)]
        builds += [(1, height + 2), (0, height + 3), ()]
        before = None
        for turn, pair in enumerate(order):
            fresh = builds[turn]
            if turn == 0:

                @pl.when(sweep > 0)
                def _():
                    for rest in range(height // 2 - 1, 1, -1):
                        take_states(sweep, rest)
                    send_halo(sweep)

            if 1 in fresh:
                wait_halo(sweep)
            if fresh:
                lift(sweep, fresh)
            if turn == len(order) - 2:

                @pl.when(sweep == 0)
                def _():
                    loads[5].wait()

            value = conv_pair(w_one, cols_one, pair)
            if turn == len(order) - 2:
                build_weight(raw_two, w_two, range(2))
            if turn == len(order) - 1:
                build_weight(raw_two, w_two, range(2, 9))
            for index in fresh:
                build(index)
            slot = 2 * (turn % 2)
            if before is not None:
                for half, index in enumerate(before):
                    activate_one(index, 2 - slot + half)
            for half, index in enumerate(pair):
                part = first[index + 1] + value[:, half * width : (half + 1) * width]
                first[index + 1] = part
                sums_one[slot + half] = part
            before, last = pair, slot

        pairs = [middle[:2], edges[:2], edges[2:]]
        pairs += [middle[place : place + 2] for place in range(2, len(middle), 2)]
        done = None
        for turn, pair in enumerate(pairs):
            value = conv_pair(w_two, cols_two, pair)
            slot = 2 * (turn % 2)
            if done is None:
                for half, index in enumerate(before):
                    activate_one(index, last + half)
            else:
                finish_pair(sweep, done, 2 - slot)
            for half, row in enumerate(pair):
                sums_two[slot + half] = (
                    first[row + 2] + value[:, half * width : (half + 1) * width]
                )
            if done is not None:
                send_drift(sweep, done[0] // 2)
            done = pair
        finish_pair(sweep, done, slot)
        send_drift(sweep, done[0] // 2)

    loads[0].wait()
    for row in range(height):
        value = x_ref[:, row, :]
        rows_f32[row] = value
        state_rows[row] = value
        xb_rows[0, row + 2] = value.astype(jnp.bfloat16)
    greeted = (steps - 1) + jnp.where(has_up, 1, 0) + jnp.where(has_down, 1, 0)
    pl.semaphore_wait(barrier, greeted)
    send_halo(0)
    for load in loads[1:4]:
        load.wait()
    wide = (-feats) % 128
    embed_bc[...] = jnp.transpose(
        jnp.pad(jnp.broadcast_to(embed_ref[...], (128, feats)), ((0, 0), (0, wide)))
    )[:feats]
    turned = jnp.transpose(
        jnp.pad(lift_ref[...].astype(jnp.float32), ((0, 128 - chans), (0, wide)))
    )[:feats]
    lift_rows[...] = turned.astype(jnp.bfloat16)

    @pl.loop(0, ITERS)
    def _(sweep):
        one_sweep(sweep)

    for pair in range(height // 2):
        wait_drift(ITERS - 1, pair)
    for row in range(height):
        total = drift_out[ITERS - 1, row] + earlier(ITERS - 1, row)
        out_ref[0, :, row, :] = rows_f32[row] + total

    for sweep in range(ITERS):
        up, down = halo_copies(sweep)

        @pl.when(has_up)
        def _():
            up.wait_send()

        @pl.when(has_down)
        def _():
            down.wait_send()

        for shift in range(1, steps):
            for pair in range(height // 2):

                @pl.when(tm + shift < steps)
                def _():
                    drift_copy(sweep, shift, pair).wait_send()


def solution(mesh):
    steps, tiles = mesh.shape["tm"], mesh.shape["space"]

    def per_device(
        first_state,
        time_embed,
        drift_scale,
        state_decay,
        lift_weight,
        conv_one,
        conv_two,
        project_weight,
    ):
        chans, height, width = first_state.shape
        feats = lift_weight.shape[0]
        block, depth = 3 * feats, 9 * feats
        peers = max(steps - 1, 1)
        vmem = pl.BlockSpec(memory_space=pltpu.VMEM)
        smem = pl.BlockSpec(memory_space=pltpu.SMEM)
        hbm = pl.BlockSpec(memory_space=pltpu.HBM)
        return pl.pallas_call(
            functools.partial(kernel, steps, tiles),
            out_shape=jax.ShapeDtypeStruct((1, chans, height, width), jnp.float32),
            in_specs=[hbm, hbm, smem, smem, hbm, hbm, hbm, hbm],
            out_specs=vmem,
            scratch_shapes=[
                pltpu.VMEM((chans, height, width), jnp.float32),
                pltpu.VMEM((1, feats), jnp.float32),
                pltpu.VMEM((chans, feats), jnp.bfloat16),
                pltpu.VMEM((chans, feats), jnp.bfloat16),
                pltpu.VMEM((3, 3, feats, feats), jnp.bfloat16),
                pltpu.VMEM((3, 3, feats, feats), jnp.bfloat16),
                pltpu.VMEM((feats, depth), jnp.bfloat16),
                pltpu.VMEM((feats, depth), jnp.bfloat16),
                pltpu.VMEM((feats, 128), jnp.float32),
                pltpu.VMEM((feats, 128), jnp.bfloat16),
                pltpu.VMEM(((height + 4) * block, width), jnp.bfloat16),
                pltpu.VMEM(((height + 2) * block, width), jnp.bfloat16),
                pltpu.VMEM((height + 4, feats, width), jnp.float32),
                pltpu.VMEM((4, feats, width), jnp.float32),
                pltpu.VMEM((4, feats, width), jnp.float32),
                pltpu.VMEM((2, feats, 2 * width), jnp.bfloat16),
                pltpu.VMEM((height, chans, width), jnp.float32),
                pltpu.VMEM((height, chans, width), jnp.float32),
                pltpu.VMEM((ITERS, height + 4, chans, width), jnp.bfloat16),
                pltpu.VMEM((ITERS, height, chans, width), jnp.float32),
                pltpu.VMEM((ITERS, peers, height, chans, width), jnp.float32),
                pltpu.SemaphoreType.DMA((6,)),
                pltpu.SemaphoreType.DMA((ITERS, 2)),
                pltpu.SemaphoreType.DMA((ITERS, 2)),
                pltpu.SemaphoreType.DMA((ITERS, peers, height // 2)),
                pltpu.SemaphoreType.DMA((ITERS, peers, height // 2)),
            ],
            compiler_params=pltpu.CompilerParams(
                collective_id=0, has_side_effects=True, vmem_limit_bytes=67043328
            ),
        )(
            first_state,
            time_embed,
            drift_scale,
            state_decay,
            lift_weight.T,
            project_weight,
            conv_one,
            conv_two,
        )

    in_specs = (P(None, "space", None), P("tm", None), P("tm"), P("tm"), P(), P(), P(), P())
    return jax.shard_map(
        per_device,
        mesh=mesh,
        in_specs=in_specs,
        out_specs=P("tm", None, "space", None),
        check_vma=False,
    )
```
